32 devices in a mesh: dp: 4 (over y, core), row: 4 (over z), col: 2 (over x).
Axes of the slice: x: 2, y: 2, z: 4, core: 2. Of those that a mesh axis runs over, the one named last changes fastest.
Arguments:
- layer_input: bfloat16 [2048, 2048], P(('dp', 'row'), 'col'), may hold values from -10 to 10
- out_grad: float32 [2048, 2048], P(('dp', 'row'), 'col'), may hold values from -6 to 6
- segments: int32 [8, 256], P(('dp', 'col')), may hold values from 0 to 3, never falling along the last dimension, each value on 1 to 128 neighbouring positions
- attn_gain: float32 [2048], P('col'), may hold values from 0.1 to 1.9
- w_query: bfloat16 [2048, 2048], P('col', 'row'), may hold values from -1 to 1
- w_keyval: bfloat16 [2, 2048, 256], P(None, 'col', 'row'), may hold values from -1 to 1
- w_out: bfloat16 [2048, 2048], P('row', 'col'), may hold values from -0.5 to 0.5
- mlp_gain: float32 [2048], P('col'), may hold values from 0.1 to 1.9
- w_gate: bfloat16 [2048, 5632], P('col', 'row'), may hold values from -0.125 to 0.125
- w_up: bfloat16 [2048, 5632], P('col', 'row'), may hold values from -0.125 to 0.125
- w_down: bfloat16 [5632, 2048], P('row', 'col'), may hold values from -0.078125 to 0.078125
Outputs:
- output: bfloat16 [2048, 2048], P(('dp', 'row'), 'col')
- d_input: float32 [2048, 2048], P(('dp', 'row'), 'col')
- d_attn_gain: float32 [2048], P('col')
- d_w_query: float32 [2048, 2048], P('col', 'row')
- d_w_keyval: float32 [2, 2048, 256], P(None, 'col', 'row')
- d_w_out: float32 [2048, 2048], P('row', 'col')
- d_mlp_gain: float32 [2048], P('col')
- d_w_gate: float32 [2048, 5632], P('col', 'row')
- d_w_up: float32 [2048, 5632], P('col', 'row')
- d_w_down: float32 [5632, 2048], P('row', 'col')
The draws below stay inside these ranges and needn't reach their ends.
Inputs may be any that keep to these rules, and one draw needn't show every extreme that they name: `segments`: in each sequence the document numbers never fall, each document holds 1 to 128 tokens, and one document holds exactly 128.
All inputs are finite; a program needn't handle non-finite values.
Results may differ from the reference program's by a relative error of at most 0.012.
The reference program's roundings to bfloat16 on the way count: a program that leaves them out, or rounds other values in their place, can miss the bound.
Values may be sent and summed in bfloat16 or wider, within the bound.
No kernel may reach another device: no remote copies, remote signals or barrier semaphores. Data moves between devices by JAX's collectives and lax.ppermute only.
A program may use at most 192 MiB of HBM per device.

```python
import math
import jax
import jax.numpy as jnp
import numpy as np
from jax import lax

MODEL_WIDTH = 2048
QUERY_HEADS_TOTAL = 32
KEY_VALUE_HEADS = 4
HEAD_SIZE = 64
FF = 5632
SEQ = 256
SEQS = 8
TOKENS = 2048


def draw_layer_input(key, part):
    noise_key = jax.random.fold_in(key, 31)
    values = jnp.clip(jax.random.normal(noise_key, (TOKENS, MODEL_WIDTH), dtype=jnp.float32), -5.0, 5.0)
    return values.astype(jnp.bfloat16)


def draw_w_query(key, part):
    values = jnp.clip(jax.random.normal(jax.random.fold_in(key, 41), (MODEL_WIDTH, QUERY_HEADS_TOTAL * HEAD_SIZE), dtype=jnp.float32), -4.0, 4.0) * MODEL_WIDTH ** (-0.5)
    return values.astype(jnp.bfloat16)


def draw_w_keyval(key, part):
    values = jnp.clip(jax.random.normal(jax.random.fold_in(key, 43), (2, MODEL_WIDTH, KEY_VALUE_HEADS * HEAD_SIZE), dtype=jnp.float32), -4.0, 4.0) * MODEL_WIDTH ** (-0.5)
    return values.astype(jnp.bfloat16)


def block_levels(own_key, shape, cuts, low, top_value):
    gain = 1.0
    for axis_at, parts in cuts:
        heights = jax.random.uniform(jax.random.fold_in(jax.random.fold_in(own_key, 6), axis_at), (parts,), jnp.float32, low / len(cuts), top_value / len(cuts))
        gain = gain * jnp.repeat(jnp.exp(heights), shape[axis_at] // parts).reshape((-1,) + (1,) * (len(shape) - 1 - axis_at))
    return gain


def length_profile(count, total, most, skew):
    portions = [(1 << 20) // math.isqrt(standing ** skew) + 1 for standing in range(2, count + 1)]
    surplus, counts = total - most - (count - 1), [1] * (count - 1)
    while surplus > 0:
        free = [i for i in range(count - 1) if counts[i] < most]
        pool, left = sum([portions[i] for i in free]), surplus
        for i in free:
            more = min(most - counts[i], max(1, left * portions[i] // pool), surplus)
            counts[i] = counts[i] + more
            surplus = surplus - more
    return np.array([most] + counts)


def uneven_parts(key, count, total, limit, lean):
    if count == 2:
        one = jax.random.randint(key, (), max(1, total - limit), min(limit, total - 1) + 1)
        return jnp.stack([one, total - one])
    sizes = jnp.asarray(length_profile(count, total, limit, lean), jnp.int32)
    couples = (count - 1) // 2
    donor, sink = sizes[1:1 + 2 * couples:2], sizes[2:2 + 2 * couples:2]
    room = jnp.minimum(donor - 1, limit - sink)
    moved = jax.random.randint(jax.random.fold_in(key, 1), (couples,), 0, 1 << 20) % (room + 1)
    sizes = sizes.at[1:1 + 2 * couples:2].set(donor - moved).at[2:2 + 2 * couples:2].set(sink + moved)
    return sizes[jax.random.permutation(jax.random.fold_in(key, 2), count)]


def centred(key, shape, scale, limit, shards=(), kind=jnp.bfloat16):
    drawn = jax.random.normal(key, shape, jnp.float32) * scale
    if len(shards) > 0:
        drawn = block_levels(key, shape, shards, -0.22, 0.18) * drawn
    return jnp.clip(drawn, min=-limit, max=limit).astype(kind)


def setup_inputs(seed: int = 0) -> dict:
    key_of = jax.random.split(jax.random.key(seed), 12)
    return {
        "layer_input": draw_layer_input(jax.random.fold_in(key_of[11], 71), 0),
        "out_grad": centred(key_of[1], (TOKENS, MODEL_WIDTH), 1.0, 6.0, ((0, 16), (1, 2)), jnp.float32),
        "segments": jax.vmap(lambda own: jnp.searchsorted(jnp.cumsum(uneven_parts(own, 4, SEQ, SEQ // 2, 0)), jnp.arange(SEQ), side="right"))(jax.random.split(key_of[2], SEQS)).reshape((SEQS, SEQ)).astype(jnp.int32),
        "attn_gain": jnp.clip(1.0 + 0.18 * jax.random.normal(key_of[3], (MODEL_WIDTH,), jnp.float32), 0.1, 1.9),
        "w_query": draw_w_query(jax.random.fold_in(key_of[11], 71), 0),
        "w_keyval": draw_w_keyval(jax.random.fold_in(key_of[11], 71), 0),
        "w_out": centred(key_of[6], (QUERY_HEADS_TOTAL * HEAD_SIZE, MODEL_WIDTH), (QUERY_HEADS_TOTAL * HEAD_SIZE // 16) ** -0.5, 0.5, ((0, 4), (1, 2))),
        "mlp_gain": jnp.clip(1.0 + 0.18 * jax.random.normal(key_of[7], (MODEL_WIDTH,), jnp.float32), 0.1, 1.9),
        "w_gate": centred(key_of[8], (MODEL_WIDTH, FF), MODEL_WIDTH ** -0.5, 0.125, ((0, 2), (1, 4))),
        "w_up": centred(key_of[9], (MODEL_WIDTH, FF), MODEL_WIDTH ** -0.5, 0.125, ((0, 2), (1, 4))),
        "w_down": centred(key_of[10], (FF, MODEL_WIDTH), FF ** -0.5, 0.078125, ((0, 4), (1, 2))),
    }


EPS = 1e-05
MASK_FILL = -1e+30

def positions_of(segment_ids):
    index_all = jnp.arange(segment_ids.shape[0], dtype=jnp.int32)
    doc_start = jnp.concatenate([jnp.ones((1,), dtype=bool), segment_ids[1:] != segment_ids[:-1]])
    first_index = lax.cummax(jnp.where(doc_start, index_all, 0).astype(jnp.int32), axis=0)
    return index_all - first_index

def rotation(positions, width):
    half_width = width // 2
    inverse_freq = jnp.exp(jnp.arange(half_width, dtype=jnp.float32) * (-2.0 * math.log(10000.0) / width))
    angles = positions.astype(jnp.float32)[:, None] * inverse_freq[None, :]
    return (jnp.cos(angles)[:, None, :], jnp.sin(angles)[:, None, :])

def rotate(tensor, cosine_table, sine_table):
    half_width = tensor.shape[-1] // 2
    first_half = tensor[..., :half_width]
    second_half = tensor[..., half_width:]
    return jnp.concatenate([first_half * cosine_table - second_half * sine_table, second_half * cosine_table + first_half * sine_table], axis=-1)

def unrotate(tensor, cosine_table, sine_table):
    half_width = tensor.shape[-1] // 2
    first_half = tensor[..., :half_width]
    second_half = tensor[..., half_width:]
    return jnp.concatenate([first_half * cosine_table + second_half * sine_table, second_half * cosine_table - first_half * sine_table], axis=-1)

def mat(left, right):
    return jnp.dot(left, right, preferred_element_type=jnp.float32)

def one_sequence(seq_input, seq_grad, segment_ids, attn_gain, w_query, w_keyval, w_out, mlp_gain, w_gate, w_up, w_down):
    length = seq_input.shape[0]
    kv_heads = w_keyval.shape[2] // HEAD_SIZE
    query_heads = w_query.shape[1] // HEAD_SIZE
    group_size = query_heads // kv_heads
    scale = HEAD_SIZE ** (-0.5)
    cosine_table, sine_table = rotation(positions_of(segment_ids), HEAD_SIZE)
    stream = seq_input.astype(jnp.float32)
    inv_attn = lax.rsqrt(lax.optimization_barrier(jnp.mean(stream * stream, axis=1)) + EPS)
    unit_attn = stream * inv_attn[:, None]
    normed_attn = (unit_attn * attn_gain).astype(jnp.bfloat16)
    queries = rotate(mat(normed_attn, w_query).reshape(length, query_heads, HEAD_SIZE), cosine_table, sine_table).astype(jnp.bfloat16)
    keys = rotate(mat(normed_attn, w_keyval[0]).reshape(length, kv_heads, HEAD_SIZE), cosine_table, sine_table).astype(jnp.bfloat16)
    values = mat(normed_attn, w_keyval[1]).astype(jnp.bfloat16).reshape(length, kv_heads, HEAD_SIZE)
    query_groups = queries.reshape(length, kv_heads, group_size, HEAD_SIZE).astype(jnp.float32)
    keys_f = keys.astype(jnp.float32)
    values_f = values.astype(jnp.float32)
    index_all = jnp.arange(length, dtype=jnp.int32)
    allowed = (segment_ids[:, None] == segment_ids[None, :]) & (index_all[None, :] <= index_all[:, None])
    scores = jnp.einsum('qkgd,tkd->kgqt', query_groups, keys_f) * scale
    scores = jnp.where(allowed[None, None], scores, MASK_FILL)
    top_score = lax.optimization_barrier(jnp.max(scores, axis=-1, keepdims=True))
    log_total = top_score + jnp.log(lax.optimization_barrier(jnp.sum(jnp.exp(scores - top_score), axis=-1, keepdims=True)))
    probs = jnp.exp(scores - log_total)
    probs_b = probs.astype(jnp.bfloat16).astype(jnp.float32)
    attn = jnp.einsum('kgqt,tkd->qkgd', probs_b, values_f).astype(jnp.bfloat16).reshape(length, query_heads * HEAD_SIZE)
    resid = stream + mat(attn, w_out)
    inv_mlp = lax.rsqrt(lax.optimization_barrier(jnp.mean(resid * resid, axis=1)) + EPS)
    unit_mlp = resid * inv_mlp[:, None]
    normed_mlp = (unit_mlp * mlp_gain).astype(jnp.bfloat16)
    gate = mat(normed_mlp, w_gate)
    up_part = mat(normed_mlp, w_up)
    sigma = jax.nn.sigmoid(gate)
    hidden = (gate * sigma * up_part).astype(jnp.bfloat16)
    output = (resid + mat(hidden, w_down)).astype(jnp.bfloat16)
    grad_b = seq_grad.astype(jnp.bfloat16)
    d_w_down = mat(hidden.T, grad_b)
    d_hidden = mat(grad_b, w_down.T)
    d_gate = (d_hidden * up_part * sigma * (1.0 + gate * (1.0 - sigma))).astype(jnp.bfloat16)
    d_up = (d_hidden * gate * sigma).astype(jnp.bfloat16)
    d_w_gate = mat(normed_mlp.T, d_gate)
    d_w_up = mat(normed_mlp.T, d_up)
    d_normed_mlp = mat(d_gate, w_gate.T) + mat(d_up, w_up.T)
    d_mlp_gain = lax.optimization_barrier(jnp.sum(d_normed_mlp * unit_mlp, axis=0))
    scaled_mlp = d_normed_mlp * mlp_gain
    d_resid = seq_grad + inv_mlp[:, None] * (scaled_mlp - unit_mlp * lax.optimization_barrier(jnp.mean(scaled_mlp * unit_mlp, axis=1, keepdims=True)))
    branch_b = d_resid.astype(jnp.bfloat16)
    d_w_out = mat(attn.T, branch_b)
    d_attn = mat(branch_b, w_out.T).astype(jnp.bfloat16)
    grad_groups = d_attn.reshape(length, kv_heads, group_size, HEAD_SIZE).astype(jnp.float32)
    attn_groups = attn.reshape(length, kv_heads, group_size, HEAD_SIZE).astype(jnp.float32)
    row_terms = jnp.transpose(lax.optimization_barrier(jnp.sum(grad_groups * attn_groups, axis=-1)), (1, 2, 0))[..., None]
    d_values = jnp.einsum('kgqt,qkgd->tkd', probs_b, grad_groups)
    d_probs = jnp.einsum('qkgd,tkd->kgqt', grad_groups, values_f)
    d_scores = (probs * (d_probs - row_terms) * scale).astype(jnp.bfloat16).astype(jnp.float32)
    d_queries = jnp.einsum('kgqt,tkd->qkgd', d_scores, keys_f).reshape(length, query_heads, HEAD_SIZE)
    d_keys = jnp.einsum('kgqt,qkgd->tkd', d_scores, query_groups)
    d_queries = unrotate(d_queries, cosine_table, sine_table).astype(jnp.bfloat16).reshape(length, query_heads * HEAD_SIZE)
    d_keys = unrotate(d_keys, cosine_table, sine_table).astype(jnp.bfloat16).reshape(length, kv_heads * HEAD_SIZE)
    d_values = d_values.astype(jnp.bfloat16).reshape(length, kv_heads * HEAD_SIZE)
    d_w_query = mat(normed_attn.T, d_queries)
    d_w_keyval = jnp.stack([mat(normed_attn.T, d_keys), mat(normed_attn.T, d_values)])
    d_normed_attn = mat(d_queries, w_query.T) + mat(d_keys, w_keyval[0].T) + mat(d_values, w_keyval[1].T)
    d_attn_gain = lax.optimization_barrier(jnp.sum(d_normed_attn * unit_attn, axis=0))
    scaled_attn = d_normed_attn * attn_gain
    d_input = d_resid + inv_attn[:, None] * (scaled_attn - unit_attn * lax.optimization_barrier(jnp.mean(scaled_attn * unit_attn, axis=1, keepdims=True)))
    grads = (d_attn_gain, d_w_query, d_w_keyval, d_w_out, d_mlp_gain, d_w_gate, d_w_up, d_w_down)
    return (output, d_input, grads)

def reference(layer_input, out_grad, segments, attn_gain, w_query, w_keyval, w_out, mlp_gain, w_gate, w_up, w_down):
    inputs_seq = layer_input.reshape(SEQS, SEQ, MODEL_WIDTH)
    grads_seq = out_grad.reshape(SEQS, SEQ, MODEL_WIDTH)
    params = (attn_gain, w_query, w_keyval, w_out, mlp_gain, w_gate, w_up, w_down)
    start_sums = tuple((jnp.zeros(param.shape, jnp.float32) for param in params))

    def step(carry, item):
        seq_input, seq_grad, segment_ids = item
        output, d_input, grads = one_sequence(seq_input, seq_grad, segment_ids, *params)
        return (tuple((running + update for running, update in zip(carry, grads))), (output, d_input))
    totals, (outputs, d_inputs) = lax.scan(step, start_sums, (inputs_seq, grads_seq, segments))
    return (outputs.reshape(TOKENS, MODEL_WIDTH), d_inputs.reshape(TOKENS, MODEL_WIDTH), totals[0], totals[1], totals[2], totals[3], totals[4], totals[5], totals[6], totals[7])
```

```python
import math

import jax
import jax.numpy as jnp
from jax import lax
from jax.sharding import PartitionSpec as P

HEAD = 64
EPS = 1e-05
MASK_FILL = -1e30
BF = jnp.bfloat16
F32 = jnp.float32


def mm(left, right):
    return jnp.dot(left, right, preferred_element_type=F32)


def mm_tn(left, right):
    return lax.dot_general(left, right, (((0,), (0,)), ((), ())), preferred_element_type=F32)


def mm_nt(left, right):
    return lax.dot_general(left, right, (((1,), (1,)), ((), ())), preferred_element_type=F32)


def after(value, *others):
    return lax.optimization_barrier((value, *others))[0]


def positions_of(segment_ids):
    index_all = jnp.arange(segment_ids.shape[0], dtype=jnp.int32)
    doc_start = jnp.concatenate([jnp.ones((1,), dtype=bool), segment_ids[1:] != segment_ids[:-1]])
    first_index = lax.cummax(jnp.where(doc_start, index_all, 0), axis=0)
    return index_all - first_index


def rotation(positions):
    inverse_freq = jnp.exp(
        jnp.arange(HEAD // 2, dtype=F32) * (-2.0 * math.log(10000.0) / HEAD)
    )
    angles = positions.astype(F32)[:, None] * inverse_freq[None, :]
    return (jnp.cos(angles)[:, None, :], jnp.sin(angles)[:, None, :])


def rotate(tensor, cosine, sine):
    a, b = tensor[..., : HEAD // 2], tensor[..., HEAD // 2 :]
    return jnp.concatenate([a * cosine - b * sine, b * cosine + a * sine], axis=-1)


def attention_forward(queries, keys, values, mask, scale):
    scores = jnp.einsum("qkgd,tkd->kgqt", queries, keys, preferred_element_type=F32) * scale
    scores = jnp.where(mask[None, None], scores, MASK_FILL)
    top = jnp.max(scores, axis=-1, keepdims=True)
    lse = top + jnp.log(jnp.sum(jnp.exp(scores - top), axis=-1, keepdims=True))
    probs = jnp.exp(scores - lse)
    mixed = jnp.einsum("kgqt,tkd->qkgd", probs.astype(BF), values, preferred_element_type=F32)
    return mixed.astype(BF), lse


def attention_backward(queries, keys, values, mask, scale, lse, d_mixed, mixed):
    terms = jnp.transpose(
        jnp.sum(d_mixed.astype(F32) * mixed.astype(F32), axis=-1), (1, 2, 0)
    )[..., None]
    scores = jnp.einsum("qkgd,tkd->kgqt", queries, keys, preferred_element_type=F32) * scale
    probs = jnp.exp(jnp.where(mask[None, None], scores, MASK_FILL) - lse)
    d_values = jnp.einsum("kgqt,qkgd->tkd", probs.astype(BF), d_mixed, preferred_element_type=F32)
    d_probs = jnp.einsum("qkgd,tkd->kgqt", d_mixed, values, preferred_element_type=F32)
    d_scores = (probs * (d_probs - terms) * scale).astype(BF)
    d_queries = jnp.einsum("kgqt,tkd->qkgd", d_scores, keys, preferred_element_type=F32)
    d_keys = jnp.einsum("kgqt,qkgd->tkd", d_scores, queries, preferred_element_type=F32)
    return d_queries, d_keys, d_values


def layer(mesh_sizes, layer_input, out_grad, segments, attn_gain, w_query, w_keyval, w_out, mlp_gain, w_gate, w_up, w_down):
    dp_size = mesh_sizes["dp"]
    d, r, c = lax.axis_index("dp"), lax.axis_index("row"), lax.axis_index("col")
    k = d % 2
    first_core = k == 0
    x_pairs = [(0, 1), (1, 0)]

    def over_x(v):
        return lax.ppermute(v, "col", x_pairs)

    def over_row(v, bit):
        return lax.ppermute(v, "row", [(i, i ^ bit) for i in range(4)])

    def over_dp(v, bit):
        return lax.ppermute(v, "dp", [(i, i ^ bit) for i in range(dp_size)])

    def dp_bits():
        bit = 2
        while bit < dp_size:
            yield bit
            bit *= 2

    def row_slots(v):
        return [v] + [over_row(v, s) for s in (1, 2, 3)]

    def assemble(slots, e):
        e0, e1 = (e & 1) == 1, (e >> 1) == 1
        return jnp.concatenate(
            [
                jnp.where(
                    e1,
                    jnp.where(e0, slots[m ^ 3], slots[m ^ 2]),
                    jnp.where(e0, slots[m ^ 1], slots[m]),
                )
                for m in range(4)
            ],
            axis=0,
        )

    def row_scatter(blocks, e):
        rows = blocks[0].shape[0] // 4

        def chunk(s):
            return jnp.concatenate(
                [lax.dynamic_slice_in_dim(b, (e ^ s) * rows, rows, 0) for b in blocks], axis=1
            )

        got = [over_row(chunk(s).astype(BF), s) for s in (3, 2, 1)]
        return chunk(0) + got[0].astype(F32) + got[1].astype(F32) + got[2].astype(F32)

    def halves(v, axis, size):
        return (
            lax.dynamic_slice_in_dim(v, k * size, size, axis),
            lax.dynamic_slice_in_dim(v, (1 - k) * size, size, axis),
        )

    def core_order(v, axis):
        size = v.shape[axis] // 2
        lo, hi = lax.slice_in_dim(v, 0, size, axis=axis), lax.slice_in_dim(v, size, 2 * size, axis=axis)
        return jnp.where(first_core, v, jnp.concatenate([hi, lo], axis=axis))

    def dp_sum(keep, send):
        total = keep + over_dp(send.astype(BF), 1).astype(F32)
        mine = total
        for bit in dp_bits():
            rounded = total.astype(BF)
            total = rounded.astype(F32) + over_dp(rounded, bit).astype(F32)
        rounded = total.astype(BF)
        return mine, rounded, over_dp(rounded, 1)

    def join(own, other, axis):
        return jnp.concatenate(
            [jnp.where(first_core, own, other), jnp.where(first_core, other, own)], axis=axis
        ).astype(F32)

    heads = w_query.shape[1] // HEAD
    kv_heads = w_keyval.shape[2] // HEAD
    groups = heads // kv_heads
    q_width, kv_width = heads * HEAD, kv_heads * HEAD
    width = layer_input.shape[1]
    half = width // 2
    model_width = 2 * width
    scale = HEAD ** (-0.5)
    seg = segments[0]
    length = seg.shape[0]
    t_rows = length // 4
    f_rows = layer_input.shape[0]
    ef = r ^ (2 * c)

    x_all = assemble(row_slots(layer_input), ef)
    w1 = over_x(halves(w_out, 1, half)[0])
    gain_other = over_x(core_order(mlp_gain, 0))
    g_send, u_send = halves(w_gate, 0, half)[0], halves(w_up, 0, half)[0]
    quarter = half // 2
    g1a = over_x(after(g_send[:quarter], w1))
    w2 = over_dp(w1, 1)

    w_inner = jnp.concatenate([w_query, w_keyval[0], w_keyval[1]], axis=1)
    x_f = x_all.astype(F32)
    squares = jnp.sum(x_f * x_f, axis=1)
    scaled_in = (x_f * attn_gain).astype(BF)
    inner = mm(scaled_in, w_inner)
    squares_x = over_x(squares)
    inner_x = over_x(inner[length:].astype(BF))
    inv_all = lax.rsqrt(
        (squares + jnp.concatenate([squares_x[length:], squares_x[:length]])) / model_width + EPS
    )
    projected = (inner[:length] + inner_x.astype(F32)) * inv_all[:length, None]
    normed_all = (x_f * inv_all[:, None] * attn_gain).astype(BF)

    grad_all = assemble(row_slots(after(out_grad.astype(BF), x_all)), ef)
    g1b = over_x(after(g_send[quarter:], inner_x))
    u1 = over_x(after(u_send, inner_x))
    d_hidden_part = mm_nt(grad_all, w_down)
    d_hidden_x = over_x(after(d_hidden_part[length:].astype(BF), g1b))
    g1 = jnp.concatenate([g1a, g1b], axis=0)
    g2 = over_dp(g1, 1)
    u2 = over_dp(u1, 1)
    d_hidden = d_hidden_part[:length] + d_hidden_x.astype(F32)

    def to_t(v_all):
        own = lax.dynamic_slice_in_dim(v_all[:length], r * t_rows, t_rows, 0)
        other = lax.dynamic_slice_in_dim(v_all[length:], r * t_rows, t_rows, 0)
        return own, over_x(core_order(other, 1))

    x_t_own, x_t_other = to_t(x_all)
    g_t_own, g_t_other = to_t(grad_all)
    x_t = jnp.concatenate([x_t_own, x_t_other], axis=1).astype(F32)
    g_t = jnp.concatenate([g_t_own, g_t_other], axis=1).astype(F32)
    gain_t = jnp.concatenate([mlp_gain, gain_other])

    cosine, sine = rotation(positions_of(seg))
    index = jnp.arange(length, dtype=jnp.int32)
    mask = (seg[:, None] == seg[None, :]) & (index[None, :] <= index[:, None])
    queries = rotate(projected[:, :q_width].reshape(length, heads, HEAD), cosine, sine).astype(BF)
    queries = queries.reshape(length, kv_heads, groups, HEAD)
    keys = rotate(
        projected[:, q_width : q_width + kv_width].reshape(length, kv_heads, HEAD), cosine, sine
    ).astype(BF)
    values = projected[:, q_width + kv_width :].astype(BF).reshape(length, kv_heads, HEAD)
    mixed, lse = attention_forward(queries, keys, values, mask, scale)
    attn = mixed.reshape(length, q_width)

    attn_proj = row_scatter([mm(attn, w_out), mm(attn, w1), mm(attn, w2)], r)
    attn_x = over_x(attn)
    resid = x_t + attn_proj
    inv_mlp = lax.rsqrt(jnp.sum(resid * resid, axis=1, keepdims=True) / model_width + EPS)
    unit_mlp = resid * inv_mlp
    normed_mlp = (unit_mlp * gain_t).astype(BF)
    n_all = assemble(row_slots(normed_mlp), r)
    n_own, n_1, n_2 = n_all[:, :width], n_all[:, width : width + half], n_all[:, width + half :]
    gate = mm(n_own, w_gate) + mm(n_1, g1) + mm(n_2, g2)
    up = mm(n_own, w_up) + mm(n_1, u1) + mm(n_2, u2)
    sigma = jax.nn.sigmoid(gate)
    hidden = (gate * sigma * up).astype(BF)
    d_gate = (d_hidden * up * sigma * (1.0 + gate * (1.0 - sigma))).astype(BF)
    d_up = (d_hidden * gate * sigma).astype(BF)

    d_norm_mlp = row_scatter(
        [
            mm_nt(d_gate, w_gate) + mm_nt(d_up, w_up),
            mm_nt(d_gate, g1) + mm_nt(d_up, u1),
            mm_nt(d_gate, g2) + mm_nt(d_up, u2),
        ],
        r,
    )
    hidden_x = over_x(hidden)
    d_gate_x = over_x(d_gate)
    d_up_x = over_x(d_up)
    n_x = over_x(n_all[:, width:])

    scaled = d_norm_mlp * gain_t
    inner_mean = jnp.sum(scaled * unit_mlp, axis=1, keepdims=True) / model_width
    d_resid = g_t + inv_mlp * (scaled - unit_mlp * inner_mean)
    branch = d_resid.astype(BF)
    b_all = assemble(row_slots(branch), r)
    b_own, b_1, b_2 = b_all[:, :width], b_all[:, width : width + half], b_all[:, width + half :]
    d_attn = (mm_nt(b_own, w_out) + mm_nt(b_1, w1) + mm_nt(b_2, w2)).astype(BF)
    b_x = over_x(b_all[:, width:])

    d_q, d_k, d_v = attention_backward(
        queries, keys, values, mask, scale, lse, d_attn.reshape(mixed.shape), mixed
    )
    d_q = rotate(d_q.reshape(length, heads, HEAD), cosine, -sine).astype(BF)
    d_k = rotate(d_k, cosine, -sine).astype(BF)
    d_inner = jnp.concatenate(
        [
            d_q.reshape(length, q_width),
            d_k.reshape(length, kv_width),
            d_v.astype(BF).reshape(length, kv_width),
        ],
        axis=1,
    )
    d_inner_x = over_x(d_inner)
    d_inner_all = jnp.concatenate([d_inner, d_inner_x], axis=0)
    d_norm_attn = row_scatter([mm_nt(d_inner_all, w_inner)], ef)

    hidden_all = jnp.concatenate([hidden, hidden_x], axis=0)
    d_gate_all = jnp.concatenate([d_gate, d_gate_x], axis=0)
    d_up_all = jnp.concatenate([d_up, d_up_x], axis=0)
    attn_all = jnp.concatenate([attn, attn_x], axis=0)
    grad_k, grad_o = halves(grad_all, 1, half)
    down_sum = dp_sum(mm_tn(hidden_all, grad_k), mm_tn(hidden_all, grad_o))
    nk, no = halves(n_own, 1, half)
    nk = jnp.concatenate([nk, n_x[:, :half]], axis=0)
    no = jnp.concatenate([no, n_x[:, half:]], axis=0)
    gate_sum = dp_sum(mm_tn(nk, d_gate_all), mm_tn(no, d_gate_all))
    up_sum = dp_sum(mm_tn(nk, d_up_all), mm_tn(no, d_up_all))
    bk, bo = halves(b_own, 1, half)
    bk = jnp.concatenate([bk, b_x[:, :half]], axis=0)
    bo = jnp.concatenate([bo, b_x[:, half:]], axis=0)
    out_sum = dp_sum(mm_tn(attn_all, bk), mm_tn(attn_all, bo))
    ak, ao = halves(normed_all, 1, half)
    inner_sum = dp_sum(mm_tn(ak, d_inner_all), mm_tn(ao, d_inner_all))

    out_part = mm(hidden_all, w_down) + mm(attn_all, w_out)
    output = (layer_input.astype(F32) + row_scatter([out_part], ef)).astype(BF)

    def butterfly(v, bits):
        for bit in (1, 2):
            v = v + over_row(v, bit)
        for bit in bits:
            v = v + over_dp(v, bit)
        return v

    gain_part = jnp.sum(d_norm_mlp * unit_mlp, axis=0)
    gain_x = core_order(over_x(gain_part[width:]), 0)
    d_mlp_gain = butterfly(gain_part[:width] + gain_x, [1, *dp_bits()])
    w_inner_k = halves(w_inner, 0, half)[0].astype(F32)
    gain_k = halves(attn_gain, 0, half)[0]
    attn_gain_part = butterfly(jnp.sum(w_inner_k * inner_sum[0], axis=1) / gain_k, dp_bits())
    d_attn_gain = join(attn_gain_part, over_dp(attn_gain_part, 1), 0)

    h_rows = (r % 2) * f_rows
    mine = lax.dynamic_slice_in_dim(b_own, h_rows, f_rows, 0)
    theirs = core_order(lax.dynamic_slice_in_dim(b_x, h_rows, f_rows, 0), 1)
    d_resid_f = jnp.where((r // 2) == c, mine, theirs).astype(F32)
    inv_f = lax.dynamic_slice_in_dim(inv_all, ef * f_rows, f_rows, 0)[:, None]
    unit_f = layer_input.astype(F32) * inv_f
    scaled_f = d_norm_attn * attn_gain
    part = jnp.sum(scaled_f * unit_f, axis=1)
    inner_f = (part + over_x(part))[:, None] / model_width
    d_input = d_resid_f + inv_f * (scaled_f - unit_f * inner_f)

    d_w_inner = join(inner_sum[1], inner_sum[2], 0)
    return (
        output,
        d_input,
        d_attn_gain,
        d_w_inner[:, :q_width],
        jnp.stack([d_w_inner[:, q_width : q_width + kv_width], d_w_inner[:, q_width + kv_width :]]),
        join(out_sum[1], out_sum[2], 1),
        d_mlp_gain,
        join(gate_sum[1], gate_sum[2], 0),
        join(up_sum[1], up_sum[2], 0),
        join(down_sum[1], down_sum[2], 1),
    )


def solution(mesh):
    sizes = dict(mesh.shape)
    assert sizes["row"] == 4 and sizes["col"] == 2

    def shards(*args):
        return layer(sizes, *args)

    in_specs = (
        P(("dp", "row"), "col"),
        P(("dp", "row"), "col"),
        P(("dp", "col"), None),
        P("col"),
        P("col", "row"),
        P(None, "col", "row"),
        P("row", "col"),
        P("col"),
        P("col", "row"),
        P("col", "row"),
        P("row", "col"),
    )
    out_specs = (
        P(("dp", "row"), "col"),
        P(("dp", "row"), "col"),
        P("col"),
        P("col", "row"),
        P(None, "col", "row"),
        P("row", "col"),
        P("col"),
        P("col", "row"),
        P("col", "row"),
        P("row", "col"),
    )
    return jax.shard_map(shards, mesh=mesh, in_specs=in_specs, out_specs=out_specs, check_vma=False)
```
